32 devices in a mesh: dp: 4 (over z), mp: 8 (over y, x, core).
Axes of the slice: x: 2, y: 2, z: 4, core: 2. Of those that a mesh axis runs over, the one named last changes fastest.
Arguments:
- hidden_in: bfloat16 [64, 8192], P(None, 'dp'), may hold values from -25 to 25
- norm_gain: bfloat16 [8192], P('dp'), may hold values from 0.099609375 to 1.8984375
- w_query: bfloat16 [8192, 8192], P('dp', 'mp'), may hold values from -0.0625 to 0.0625
- w_keyval: bfloat16 [8192, 2048], P('dp', 'mp'), may hold values from -0.25 to 0.25
- w_out: bfloat16 [8192, 8192], P('mp', 'dp'), may hold values from -0.5 to 0.5
- cache_slots: bfloat16 [2, 64, 2, 8, 512, 128], P(None, ('dp', 'mp')), may hold values from -140 to 140
- lengths: int32 [64], replicated, may hold values from 1 to 512, 16384 in all
- positions: int32 [64], replicated, may hold values from 0 to 8191
- slot_order: int32 [64], replicated, may hold values from 0 to 63, each once
Outputs:
- result: bfloat16 [64, 8192], P(None, 'dp')
The draws below stay inside these ranges and needn't reach their ends.
Inputs may be any that keep to these rules, and one draw needn't show every extreme that they name: `lengths`: every request has at least one valid cache position; the longest has 512. `slot_order`: each request's cache sits in exactly one slot.
All inputs are finite; a program needn't handle non-finite values.
Results may differ from the reference program's by a relative error of at most 0.035.
Values may be sent and summed in bfloat16 or wider, within the bound.
A program may use at most 128 MiB of HBM per device.

```python
import math
import jax
import jax.numpy as jnp
import numpy as np
from jax import lax

D = 8192
HEADS = 64
KV_HEADS = 8
HEAD_DIM = 128
LAYERS = 2
CACHE = 512
REQUESTS = 64


def draw_hidden_in(key, part):
    first_key, second_key = jax.random.split(key)
    array_shape = (REQUESTS, D)
    columns = 1.0 + 0.8 * lax.broadcasted_iota(jnp.float32, (1, D), 1) / D
    base_draw = jnp.clip(jax.random.normal(first_key, array_shape, jnp.float32), -4.0, 4.0)
    row_scale = jnp.exp(jax.random.uniform(second_key, (REQUESTS, 1), jnp.float32, math.log(0.3), math.log(3.0)))
    return (base_draw * row_scale * columns).astype(jnp.bfloat16)


def draw_cache_slots(key, part):
    array_shape = (LAYERS, REQUESTS, 2, KV_HEADS, CACHE, HEAD_DIM)
    kind_index = lax.broadcasted_iota(jnp.int32, array_shape, 2)
    base_draw = jnp.clip(jax.random.normal(key, array_shape, jnp.float32), -6.0, 6.0)
    key_rows = 2.0 * base_draw
    return jnp.where(kind_index == 0, key_rows, base_draw).astype(jnp.bfloat16)


def touch_ends(entries, own_key, smallest, high):
    index_at = [jax.random.randint(jax.random.fold_in(own_key, axis), (), 0, length) for axis, length in enumerate(entries.shape)]
    main_axis = entries.shape.index(max(entries.shape))
    beside = index_at[:main_axis] + [(index_at[main_axis] + 1) % entries.shape[main_axis]] + index_at[main_axis + 1:]
    return entries.at[tuple(index_at)].set(smallest).at[tuple(beside)].set(high)


def level_of(rng, extent, cuts, smallest, largest):
    def one(position, blocks):
        steps = jax.random.uniform(jax.random.fold_in(jax.random.fold_in(rng, 6), position), (blocks,), jnp.float32, smallest / len(cuts), largest / len(cuts))
        return jnp.repeat(jnp.exp(steps), extent[position] // blocks).reshape((-1,) + (1,) * (len(extent) - position - 1))

    gain = one(*cuts[0])
    for cut in cuts[1:]:
        gain = gain * one(*cut)
    return gain


def length_profile(count, total, bound, lean):
    loads = [(1 << 20) // math.isqrt(grade ** lean) + 1 for grade in range(2, count + 1)]
    spare, given = total - bound - (count - 1), [1] * (count - 1)
    while spare > 0:
        free = [i for i in range(count - 1) if given[i] < bound]
        whole, left = sum([loads[i] for i in free]), spare
        for i in free:
            extra = min(bound - given[i], max(1, left * loads[i] // whole), spare)
            given[i] = given[i] + extra
            spare = spare - extra
    return np.array([bound] + given)


def uneven(rng, amount, total, limit, skew):
    if amount == 2:
        one = jax.random.randint(rng, (), max(1, total - limit), min(limit, total - 1) + 1)
        return jnp.stack([one, total - one])
    sizes = jnp.asarray(length_profile(amount, total, limit, skew), jnp.int32)
    couples = (amount - 1) // 2
    giver, receiver = sizes[1:1 + 2 * couples:2], sizes[2:2 + 2 * couples:2]
    room = jnp.minimum(giver - 1, limit - receiver)
    passed = jax.random.randint(jax.random.fold_in(rng, 1), (couples,), 0, 1 << 20) % (room + 1)
    sizes = sizes.at[1:1 + 2 * couples:2].set(giver - passed).at[2:2 + 2 * couples:2].set(receiver + passed)
    return sizes[jax.random.permutation(jax.random.fold_in(rng, 2), amount)]


def centred(rng, shape, deviation, limit, cuts=(), kind=jnp.bfloat16):
    drawn = jax.random.normal(rng, shape, jnp.float32) * deviation
    if len(cuts) > 0:
        drawn = level_of(rng, shape, cuts, -0.22, 0.18) * drawn
    return jnp.clip(drawn, min=-limit, max=limit).astype(kind)


def setup_inputs(seed: int = 0) -> dict:
    key_of = jax.random.split(jax.random.key(seed), 10)
    hidden_in = draw_hidden_in(jax.random.fold_in(key_of[9], 71), 0)
    norm_gain = jnp.clip(1.0 + 0.18 * jax.random.normal(key_of[1], (D,), jnp.float32), 0.099609375, 1.8984375).astype(jnp.bfloat16)
    w_query = centred(key_of[2], (D, HEADS * HEAD_DIM), D ** -0.5, 0.0625, ((0, 4), (1, 8)))
    w_keyval = centred(key_of[3], (D, 2 * KV_HEADS * HEAD_DIM), (D // 16) ** -0.5, 0.25, ((0, 4), (1, 8)))
    w_out = centred(key_of[4], (HEADS * HEAD_DIM, D), HEAD_DIM ** -0.5, 0.5, ((0, 8), (1, 4)))
    cache_slots = draw_cache_slots(jax.random.fold_in(key_of[9], 71), 0)
    lengths = uneven(key_of[6], REQUESTS, REQUESTS * CACHE // 2, CACHE, 2).astype(jnp.int32)
    positions = touch_ends(jax.random.randint(key_of[7], (REQUESTS,), 0, 8192), jax.random.fold_in(key_of[7], 1), 0, 8191).astype(jnp.int32)
    slot_order = jax.random.permutation(key_of[8], REQUESTS).astype(jnp.int32)
    return {"hidden_in": hidden_in, "norm_gain": norm_gain, "w_query": w_query, "w_keyval": w_keyval, "w_out": w_out, "cache_slots": cache_slots, "lengths": lengths, "positions": positions, "slot_order": slot_order}


norm_eps = 1e-05
rope_base = 500000.0

def rotate(values, at_positions):
    half_dim = values.shape[-1] // 2
    index_row = jnp.arange(half_dim, dtype=jnp.float32)
    frequency = jnp.exp(index_row * (-2.0 * math.log(rope_base) / values.shape[-1]))
    angles = at_positions.astype(jnp.float32)[:, None, None] * frequency
    cosines = jnp.cos(angles)
    sine_rows = jnp.sin(angles)
    first_half = values[..., :half_dim]
    second_half = values[..., half_dim:]
    return jnp.concatenate([first_half * cosines - second_half * sine_rows, second_half * cosines + first_half * sine_rows], axis=-1)

def attend_slot(pieces):
    query_row, key_fresh, value_fresh, length_one, slot_cache = pieces
    group_size = HEADS // KV_HEADS
    queries = query_row.reshape(KV_HEADS, group_size, HEAD_DIM).astype(jnp.float32)
    key_rows = slot_cache[0].astype(jnp.float32)
    values = slot_cache[1].astype(jnp.float32)
    score_scale = 1.0 / math.sqrt(HEAD_DIM)
    scores = jnp.einsum('kgd,ktd->kgt', queries, key_rows) * score_scale
    own_score = jnp.einsum('kgd,kd->kg', queries, key_fresh.astype(jnp.float32)) * score_scale
    valid_keys = jnp.arange(CACHE, dtype=jnp.int32) < length_one
    scores = jnp.where(valid_keys[None, None, :], scores, -jnp.inf)
    highest = jnp.maximum(lax.optimization_barrier(jnp.max(scores, axis=-1)), own_score)
    weights = jnp.exp(scores - highest[..., None])
    own_weight = jnp.exp(own_score - highest)
    denominator = lax.optimization_barrier(jnp.sum(weights, axis=-1)) + own_weight
    rounded = lax.optimization_barrier(weights.astype(jnp.bfloat16)).astype(jnp.float32)
    own_rounded = lax.optimization_barrier(own_weight.astype(jnp.bfloat16)).astype(jnp.float32)
    summed = jnp.einsum('kgt,ktd->kgd', rounded, values) + own_rounded[..., None] * value_fresh.astype(jnp.float32)[:, None, :]
    return (summed / denominator[..., None]).reshape(HEADS * HEAD_DIM).astype(jnp.bfloat16)

def reference(hidden_in, norm_gain, w_query, w_keyval, w_out, cache_slots, lengths, positions, slot_order):
    request_count = hidden_in.shape[0]
    inverse = jnp.zeros((request_count,), jnp.int32).at[slot_order].set(jnp.arange(request_count, dtype=jnp.int32))
    current = hidden_in
    half_width = KV_HEADS * HEAD_DIM
    for layer_index in range(LAYERS):
        floats = current.astype(jnp.float32)
        inverse_rms = lax.rsqrt(lax.optimization_barrier(jnp.sum(floats * floats, axis=1)) / D + norm_eps)
        scaled = (floats * norm_gain.astype(jnp.float32)).astype(jnp.bfloat16)
        query_raw = jnp.dot(scaled, w_query, preferred_element_type=jnp.float32) * inverse_rms[:, None]
        keyval_raw = jnp.dot(scaled, w_keyval, preferred_element_type=jnp.float32) * inverse_rms[:, None]
        queries = rotate(query_raw.reshape(request_count, HEADS, HEAD_DIM), positions).astype(jnp.bfloat16)
        fresh_keys = rotate(keyval_raw[:, :half_width].reshape(request_count, KV_HEADS, HEAD_DIM), positions).astype(jnp.bfloat16)
        fresh_values = keyval_raw[:, half_width:].reshape(request_count, KV_HEADS, HEAD_DIM).astype(jnp.bfloat16)
        slot_out = lax.map(attend_slot, (jnp.take(queries, slot_order, axis=0), jnp.take(fresh_keys, slot_order, axis=0), jnp.take(fresh_values, slot_order, axis=0), jnp.take(lengths, slot_order), cache_slots[layer_index]))
        attended = jnp.take(slot_out, inverse, axis=0)
        projected = jnp.dot(attended, w_out, preferred_element_type=jnp.float32)
        current = (floats + projected).astype(jnp.bfloat16)
    return current
```

```python
import functools
import math

import jax
import jax.numpy as jnp
from jax import lax
from jax.experimental import pallas as pl
from jax.experimental.pallas import tpu as pltpu
from jax.sharding import PartitionSpec as P

LAYERS = 2


norm_eps = 1e-05
rope_base = 500000.0


def rotate(values, at_positions):
    half_dim = values.shape[-1] // 2
    index_row = jnp.arange(half_dim, dtype=jnp.float32)
    frequency = jnp.exp(index_row * (-2.0 * math.log(rope_base) / values.shape[-1]))
    angles = at_positions.astype(jnp.float32)[:, None, None] * frequency
    cosines = jnp.cos(angles)
    sine_rows = jnp.sin(angles)
    first_half = values[..., :half_dim]
    second_half = values[..., half_dim:]
    return jnp.concatenate(
        [
            first_half * cosines - second_half * sine_rows,
            second_half * cosines + first_half * sine_rows,
        ],
        axis=-1,
    )


def attend(queries, fresh_keys, fresh_values, key_rows, values, slot_lengths):
    score_scale = 1.0 / math.sqrt(queries.shape[-1])
    scores = (
        jnp.einsum("rkgd,rktd->rkgt", queries, key_rows, preferred_element_type=jnp.float32)
        * score_scale
    )
    own_score = (
        jnp.einsum("rkgd,rkd->rkg", queries, fresh_keys, preferred_element_type=jnp.float32)
        * score_scale
    )
    positions_row = lax.broadcasted_iota(jnp.int32, (1, 1, 1, key_rows.shape[2]), 3)
    valid_keys = positions_row < slot_lengths[:, None, None, None]
    scores = jnp.where(valid_keys, scores, -jnp.inf)
    highest = jnp.maximum(jnp.max(scores, axis=-1), own_score)
    weights = jnp.exp(scores - highest[..., None])
    own_weight = jnp.exp(own_score - highest)
    denominator = jnp.sum(weights, axis=-1) + own_weight
    rounded = weights.astype(jnp.bfloat16)
    own_rounded = lax.optimization_barrier(own_weight.astype(jnp.bfloat16)).astype(jnp.float32)
    summed = jnp.einsum("rkgt,rktd->rkgd", rounded, values, preferred_element_type=jnp.float32)
    summed = summed + own_rounded[..., None] * fresh_values.astype(jnp.float32)[:, :, None, :]
    return (summed / denominator[..., None]).astype(jnp.bfloat16)


def shards(
    hidden_in, norm_gain, w_query, w_keyval, w_out, cache_slots, lengths, positions, slot_order
):
    total_rows = hidden_in.shape[0]
    data_count = lax.axis_size("dp")
    model_count = lax.axis_size("mp")
    owned_rows = cache_slots.shape[1]
    key_heads = cache_slots.shape[3]
    head_dim = cache_slots.shape[5]
    query_cols = w_query.shape[1]
    head_count = query_cols * model_count // head_dim
    group_size = head_count // key_heads
    model_width = hidden_in.shape[1] * data_count
    half_width = key_heads * head_dim
    inverse = (
        jnp.zeros((total_rows,), jnp.int32)
        .at[slot_order]
        .set(jnp.arange(total_rows, dtype=jnp.int32))
    )
    device_index = lax.axis_index("dp") * model_count + lax.axis_index("mp")
    slot_lengths = lax.dynamic_slice_in_dim(
        jnp.take(lengths, slot_order), device_index * owned_rows, owned_rows
    )
    slot_positions = lax.dynamic_slice_in_dim(
        jnp.take(positions, slot_order), device_index * owned_rows, owned_rows
    )
    gain_float = norm_gain.astype(jnp.float32)
    current = jnp.take(hidden_in, slot_order, axis=0)
    for layer_index in range(LAYERS):
        floats = current.astype(jnp.float32)
        squares = jnp.sum(floats * floats, axis=1)
        scaled = (floats * gain_float).astype(jnp.bfloat16)
        partial_value = jnp.concatenate(
            [
                jnp.dot(scaled, w_query, preferred_element_type=jnp.float32),
                jnp.dot(scaled, w_keyval, preferred_element_type=jnp.float32),
            ],
            axis=1,
        )
        summed = lax.psum_scatter(partial_value, "dp", scatter_dimension=0, tiled=True)
        square_sum = lax.psum_scatter(squares, "dp", scatter_dimension=0, tiled=True)
        inverse_rms = lax.rsqrt(square_sum / model_width + norm_eps)
        projected = summed * inverse_rms[:, None]
        arrived = lax.all_to_all(projected, "mp", split_axis=0, concat_axis=1, tiled=True)
        arrived = arrived.reshape(owned_rows, model_count, projected.shape[1])
        query_part = arrived[:, :, :query_cols].reshape(owned_rows, head_count, head_dim)
        keyval_part = arrived[:, :, query_cols:].reshape(owned_rows, 2 * half_width)
        queries = (
            rotate(query_part, slot_positions)
            .astype(jnp.bfloat16)
            .reshape(owned_rows, key_heads, group_size, head_dim)
        )
        fresh_keys = rotate(
            keyval_part[:, :half_width].reshape(owned_rows, key_heads, head_dim), slot_positions
        ).astype(jnp.bfloat16)
        fresh_values = (
            keyval_part[:, half_width:]
            .reshape(owned_rows, key_heads, head_dim)
            .astype(jnp.bfloat16)
        )
        layer_cache = cache_slots[layer_index]
        attended = attend(
            queries, fresh_keys, fresh_values, layer_cache[:, 0], layer_cache[:, 1], slot_lengths
        )
        attended = attended.reshape(owned_rows, head_count * head_dim)
        returned = lax.all_to_all(attended, "mp", split_axis=1, concat_axis=0, tiled=True)
        partial_out = jnp.dot(
            lax.all_gather(returned, "dp", axis=0, tiled=True),
            w_out,
            preferred_element_type=jnp.float32,
        )
        totals = lax.psum(partial_out, "mp")
        current = (floats + totals).astype(jnp.bfloat16)
    return jnp.take(current, inverse, axis=0)


LINK = jnp.bfloat16


def fused_kernel(
    sizes,
    slot_s,
    length_s,
    slot_col,
    slot_row,
    cos_ref,
    sin_ref,
    hidden_ref,
    gain_ref,
    wq_hbm,
    wkv_hbm,
    wo_hbm,
    cache_hbm,
    out_ref,
    wq,
    wkv,
    wo,
    cache,
    state,
    scaled,
    part_own,
    square_send,
    square_recv,
    part_send,
    part_recv,
    proj_send,
    proj_recv,
    query_buf,
    fresh_buf,
    att_buf,
    att_send,
    att_recv,
    att_rows,
    gathered,
    out_own,
    out_send,
    out_recv,
    load_sem,
    sq_ssem,
    sq_rsem,
    pa_ssem,
    pa_rsem,
    pr_ssem,
    pr_rsem,
    at_ssem,
    at_rsem,
    ga_ssem,
    ga_rsem,
    ou_ssem,
    ou_rsem,
    st_ssem,
    st_rsem,
):
    n_dp, n_mp, rows, width, query_cols, keyval_cols, owned, key_heads, head_dim = sizes
    band = rows // n_dp
    chunk = width // n_mp
    group = query_cols // head_dim
    block = keyval_cols
    blocks = (query_cols + keyval_cols) // block
    d = lax.axis_index("dp")
    m = lax.axis_index("mp")
    model_width = width * n_dp
    score_scale = 1.0 / math.sqrt(head_dim)

    loads = [
        pltpu.make_async_copy(wkv_hbm, wkv, load_sem.at[0]),
        pltpu.make_async_copy(wq_hbm, wq, load_sem.at[1]),
        pltpu.make_async_copy(cache_hbm.at[0], cache.at[0], load_sem.at[2]),
    ]
    for j in range(n_mp):
        loads.append(
            pltpu.make_async_copy(
                wo_hbm.at[:, pl.ds(j * chunk, chunk)], wo.at[j], load_sem.at[3 + j]
            )
        )
    for layer in range(1, LAYERS):
        loads.append(
            pltpu.make_async_copy(
                cache_hbm.at[layer], cache.at[layer], load_sem.at[2 + n_mp + layer]
            )
        )
    for one in loads:
        one.start()

    barrier = pltpu.get_barrier_semaphore()
    for k in range(1, n_dp):
        pl.semaphore_signal(
            barrier,
            inc=1,
            device_id={"dp": lax.rem(d + k, n_dp)},
            device_id_type=pl.DeviceIdType.MESH,
        )
    for k in range(1, n_mp):
        pl.semaphore_signal(
            barrier,
            inc=1,
            device_id={"mp": lax.rem(m + k, n_mp)},
            device_id_type=pl.DeviceIdType.MESH,
        )

    lanes = lax.broadcasted_iota(jnp.int32, (rows, rows), 1)
    pick = jnp.where(slot_col[...] == lanes, 1.0, 0.0).astype(jnp.bfloat16)
    for c in range(n_mp):
        state[0, c] = jnp.dot(
            pick, hidden_ref[:, c * chunk : (c + 1) * chunk], preferred_element_type=jnp.float32
        ).astype(jnp.bfloat16)

    pl.semaphore_wait(barrier, n_dp - 1 + n_mp - 1)

    sends = []

    def remote(src, dst, ssem, rsem, where):
        copy = pltpu.make_async_remote_copy(
            src_ref=src,
            dst_ref=dst,
            send_sem=ssem,
            recv_sem=rsem,
            device_id=where,
            device_id_type=pl.DeviceIdType.MESH,
        )
        copy.start()
        sends.append(copy)
        return copy

    arriving = []
    for layer in range(LAYERS):
        for copy in arriving:
            copy.wait_recv()
        squares = jnp.zeros((rows, 128), jnp.float32)
        for c in range(n_mp):
            floats = state[layer, c].astype(jnp.float32)
            gain = gain_ref[:, c * chunk : (c + 1) * chunk].astype(jnp.float32)
            scaled[:, c * chunk : (c + 1) * chunk] = (floats * gain).astype(jnp.bfloat16)
            for t in range(chunk // 128):
                piece = floats[:, t * 128 : (t + 1) * 128]
                squares = squares + piece * piece
        square_row = jnp.sum(squares, axis=1, keepdims=True)
        square_send[layer] = jnp.broadcast_to(square_row, (rows, 128)).reshape(n_dp, band, 128)
        square_copies = []
        for k in range(1, n_dp):
            to = lax.rem(d + k, n_dp)
            square_copies.append(
                remote(
                    square_send.at[layer, to],
                    square_recv.at[layer, k - 1],
                    sq_ssem.at[layer, k - 1],
                    sq_rsem.at[layer, k - 1],
                    {"dp": to},
                )
            )
        part_copies = []
        for b in range(blocks):
            if b == 0:
                if layer == 0:
                    loads[0].wait()
                weights = wkv[...]
            else:
                if layer == 0 and b == 1:
                    loads[1].wait()
                weights = wq[:, (b - 1) * block : b * block]
            product = jnp.dot(scaled[...], weights, preferred_element_type=jnp.float32)
            product = product.reshape(n_dp, band, block)
            part_own[b] = product
            part_send[layer, b] = product.astype(LINK)
            for k in range(1, n_dp):
                to = lax.rem(d + k, n_dp)
                part_copies.append(
                    remote(
                        part_send.at[layer, b, to],
                        part_recv.at[layer, b, k - 1],
                        pa_ssem.at[layer, b, k - 1],
                        pa_rsem.at[layer, b, k - 1],
                        {"dp": to},
                    )
                )
        for copy in square_copies:
            copy.wait_recv()
        square_sum = square_send[layer, d]
        for k in range(1, n_dp):
            square_sum = square_sum + square_recv[layer, k - 1]
        inverse_rms = lax.rsqrt(square_sum / model_width + norm_eps)[:, :1]
        for copy in part_copies:
            copy.wait_recv()
        for b in range(blocks):
            total = part_own[b, d]
            for k in range(1, n_dp):
                total = total + part_recv[layer, b, k - 1].astype(jnp.float32)
            total = total * inverse_rms
            start = query_cols if b == 0 else (b - 1) * block
            for j in range(n_mp):
                proj_send[layer, j, :, start : start + block] = total[
                    j * owned : (j + 1) * owned
                ]
        proj_copies = []
        for k in range(1, n_mp):
            to = lax.rem(m + k, n_mp)
            proj_copies.append(
                remote(
                    proj_send.at[layer, to],
                    proj_recv.at[layer, m],
                    pr_ssem.at[layer, k - 1],
                    pr_rsem.at[layer, k - 1],
                    {"mp": to},
                )
            )
        proj_recv[layer, m] = proj_send[layer, m]
        for copy in proj_copies:
            copy.wait_recv()

        if layer == 0:
            loads[2].wait()
        else:
            loads[2 + n_mp + layer].wait()
        for r in range(owned):
            slot = slot_s[(d * n_mp + m) * owned + r]
            cosines = cos_ref[pl.ds(slot, 1), :]
            sines = sin_ref[pl.ds(slot, 1), :]
            length = length_s[slot]

            def turned(x):
                return x * cosines + pltpu.roll(x, head_dim // 2, 1) * sines

            for g in range(group):
                query_buf[r, :, g, :] = turned(
                    proj_recv[layer, :, r, g * head_dim : (g + 1) * head_dim]
                )
            per = keyval_cols // head_dim
            key_sources = key_heads // per
            for t in range(per):
                start = query_cols + t * head_dim
                fresh = proj_recv[layer, :, r, start : start + head_dim]
                keys_fresh = turned(fresh)
                for source in range(n_mp):
                    kind = source // key_sources
                    head = (source % key_sources) * per + t
                    row = keys_fresh if kind == 0 else fresh
                    fresh_buf[r, kind, head : head + 1, :] = row[source : source + 1]
            queries = query_buf[r].astype(jnp.bfloat16)
            fresh_keys = fresh_buf[r, 0].astype(jnp.bfloat16).astype(jnp.float32)
            fresh_values = fresh_buf[r, 1].astype(jnp.bfloat16).astype(jnp.float32)
            key_rows = cache[layer, r, 0]
            value_rows = cache[layer, r, 1]
            scores = (
                lax.dot_general(
                    queries,
                    key_rows,
                    (((2,), (2,)), ((0,), (0,))),
                    preferred_element_type=jnp.float32,
                )
                * score_scale
            )
            own_score = (
                jnp.sum(
                    queries.astype(jnp.float32) * fresh_keys[:, None, :], axis=2, keepdims=True
                )
                * score_scale
            )
            at = lax.broadcasted_iota(jnp.int32, scores.shape, 2)
            scores = jnp.where(at < length, scores, -jnp.inf)
            highest = jnp.maximum(jnp.max(scores, axis=2, keepdims=True), own_score)
            weights = jnp.exp(scores - highest)
            own_weight = jnp.exp(own_score - highest)
            denominator = jnp.sum(weights, axis=2, keepdims=True) + own_weight
            summed = lax.dot_general(
                weights.astype(jnp.bfloat16),
                value_rows,
                (((2,), (1,)), ((0,), (0,))),
                preferred_element_type=jnp.float32,
            )
            own_rounded = own_weight.astype(jnp.bfloat16).astype(jnp.float32)
            summed = summed + own_rounded * fresh_values[:, None, :]
            att_buf[r] = summed / denominator
            for g in range(group):
                att_send[layer, :, r, g * head_dim : (g + 1) * head_dim] = att_buf[r, :, g, :]
        att_copies = []
        for k in range(1, n_mp):
            to = lax.rem(m + k, n_mp)
            att_copies.append(
                remote(
                    att_send.at[layer, to],
                    att_recv.at[layer, m],
                    at_ssem.at[layer, k - 1],
                    at_rsem.at[layer, k - 1],
                    {"mp": to},
                )
            )
        att_recv[layer, m] = att_send[layer, m]
        for copy in att_copies:
            copy.wait_recv()
        for j in range(n_mp):
            att_rows[j * owned : (j + 1) * owned, :] = att_recv[layer, j]
        gathered[layer, d] = att_rows[...].astype(jnp.bfloat16)
        gather_copies = []
        for k in range(1, n_dp):
            gather_copies.append(
                remote(
                    gathered.at[layer, d],
                    gathered.at[layer, d],
                    ga_ssem.at[layer, k - 1],
                    ga_rsem.at[layer, k - 1],
                    {"dp": lax.rem(d + k, n_dp)},
                )
            )
        for copy in gather_copies:
            copy.wait_recv()
        if layer == 0:
            for j in range(n_mp):
                loads[3 + j].wait()
        left = gathered[layer].reshape(rows, query_cols)
        out_copies = []
        for k in range(1, n_mp):
            to = lax.rem(m + k, n_mp)
            product = jnp.dot(left, wo[to], preferred_element_type=jnp.float32)
            out_send[layer, k - 1] = product.astype(LINK)
            out_copies.append(
                remote(
                    out_send.at[layer, k - 1],
                    out_recv.at[layer, k - 1],
                    ou_ssem.at[layer, k - 1],
                    ou_rsem.at[layer, k - 1],
                    {"mp": to},
                )
            )
        out_own[...] = state[layer, m].astype(jnp.float32) + jnp.dot(
            left, wo[m], preferred_element_type=jnp.float32
        )
        for copy in out_copies:
            copy.wait_recv()
        total = out_own[...]
        for k in range(1, n_mp):
            total = total + out_recv[layer, k - 1].astype(jnp.float32)
        state[layer + 1, m] = total.astype(jnp.bfloat16)
        arriving = []
        for k in range(1, n_mp):
            arriving.append(
                remote(
                    state.at[layer + 1, m],
                    state.at[layer + 1, m],
                    st_ssem.at[layer, k - 1],
                    st_rsem.at[layer, k - 1],
                    {"mp": lax.rem(m + k, n_mp)},
                )
            )
    for copy in arriving:
        copy.wait_recv()
    sublanes = lax.broadcasted_iota(jnp.int32, (rows, rows), 0)
    place = jnp.where(slot_row[...] == sublanes, 1.0, 0.0).astype(jnp.bfloat16)
    for c in range(n_mp):
        out_ref[:, c * chunk : (c + 1) * chunk] = jnp.dot(
            place, state[LAYERS, c], preferred_element_type=jnp.float32
        ).astype(jnp.bfloat16)
    for copy in sends:
        copy.wait_send()


def fused(
    hidden_in, norm_gain, w_query, w_keyval, w_out, cache_slots, lengths, positions, slot_order
):
    n_dp = lax.axis_size("dp")
    n_mp = lax.axis_size("mp")
    rows, width = hidden_in.shape
    query_cols = w_query.shape[1]
    keyval_cols = w_keyval.shape[1]
    owned, key_heads, cache_rows, head_dim = (
        cache_slots.shape[1],
        cache_slots.shape[3],
        cache_slots.shape[4],
        cache_slots.shape[5],
    )
    group = query_cols // head_dim
    band = rows // n_dp
    chunk = width // n_mp
    blocks = (query_cols + keyval_cols) // keyval_cols
    half_dim = head_dim // 2
    index_row = jnp.arange(half_dim, dtype=jnp.float32)
    frequency = jnp.exp(index_row * (-2.0 * math.log(rope_base) / head_dim))
    angles = positions.astype(jnp.float32)[:, None] * jnp.concatenate([frequency, frequency])
    sign = jnp.where(jnp.arange(head_dim) < half_dim, -1.0, 1.0)
    cosines = jnp.cos(angles)
    sines = jnp.sin(angles) * sign
    sizes = (n_dp, n_mp, rows, width, query_cols, keyval_cols, owned, key_heads, head_dim)
    vmem = pl.BlockSpec(memory_space=pltpu.VMEM)
    smem = pl.BlockSpec(memory_space=pltpu.SMEM)
    anywhere = pl.BlockSpec(memory_space=pl.ANY)
    f32, bf16 = jnp.float32, jnp.bfloat16
    dma = pltpu.SemaphoreType.DMA
    return pl.pallas_call(
        functools.partial(fused_kernel, sizes),
        out_shape=jax.ShapeDtypeStruct((rows, width), bf16),
        in_specs=[smem, smem, vmem, vmem, vmem, vmem, vmem, vmem] + [anywhere] * 4,
        out_specs=vmem,
        scratch_shapes=[
            pltpu.VMEM(w_query.shape, bf16),
            pltpu.VMEM(w_keyval.shape, bf16),
            pltpu.VMEM((n_mp, query_cols, chunk), bf16),
            pltpu.VMEM(cache_slots.shape, bf16),
            pltpu.VMEM((LAYERS + 1, n_mp, rows, chunk), bf16),
            pltpu.VMEM((rows, width), bf16),
            pltpu.VMEM((blocks, n_dp, band, keyval_cols), f32),
            pltpu.VMEM((LAYERS, n_dp, band, 128), f32),
            pltpu.VMEM((LAYERS, n_dp - 1, band, 128), f32),
            pltpu.VMEM((LAYERS, blocks, n_dp, band, keyval_cols), LINK),
            pltpu.VMEM((LAYERS, blocks, n_dp - 1, band, keyval_cols), LINK),
            pltpu.VMEM((LAYERS, n_mp, owned, query_cols + keyval_cols), f32),
            pltpu.VMEM((LAYERS, n_mp, owned, query_cols + keyval_cols), f32),
            pltpu.VMEM((owned, n_mp, group, head_dim), f32),
            pltpu.VMEM((owned, 2, key_heads, head_dim), f32),
            pltpu.VMEM((owned, n_mp, group, head_dim), f32),
            pltpu.VMEM((LAYERS, n_mp, owned, query_cols), f32),
            pltpu.VMEM((LAYERS, n_mp, owned, query_cols), f32),
            pltpu.VMEM((band, query_cols), f32),
            pltpu.VMEM((LAYERS, n_dp, band, query_cols), bf16),
            pltpu.VMEM((rows, chunk), f32),
            pltpu.VMEM((LAYERS, n_mp - 1, rows, chunk), LINK),
            pltpu.VMEM((LAYERS, n_mp - 1, rows, chunk), LINK),
            dma((2 + n_mp + LAYERS,)),
            dma((LAYERS, n_dp - 1)),
            dma((LAYERS, n_dp - 1)),
            dma((LAYERS, blocks, n_dp - 1)),
            dma((LAYERS, blocks, n_dp - 1)),
            dma((LAYERS, n_mp - 1)),
            dma((LAYERS, n_mp - 1)),
            dma((LAYERS, n_mp - 1)),
            dma((LAYERS, n_mp - 1)),
            dma((LAYERS, n_dp - 1)),
            dma((LAYERS, n_dp - 1)),
            dma((LAYERS, n_mp - 1)),
            dma((LAYERS, n_mp - 1)),
            dma((LAYERS, n_mp - 1)),
            dma((LAYERS, n_mp - 1)),
        ],
        compiler_params=pltpu.CompilerParams(
            collective_id=0, has_side_effects=True, vmem_limit_bytes=56 << 20
        ),
    )(
        slot_order,
        lengths,
        slot_order.reshape(rows, 1),
        slot_order.reshape(1, rows),
        cosines,
        sines,
        hidden_in,
        norm_gain.reshape(1, width),
        w_query,
        w_keyval,
        w_out,
        cache_slots,
    )


def dispatch(
    hidden_in, norm_gain, w_query, w_keyval, w_out, cache_slots, lengths, positions, slot_order
):
    n_mp = lax.axis_size("mp")
    key_heads = cache_slots.shape[3]
    head_dim = cache_slots.shape[5]
    fits = (
        key_heads == n_mp
        and w_keyval.shape[1] % head_dim == 0
        and w_query.shape[1] % w_keyval.shape[1] == 0
        and hidden_in.shape[1] % (128 * n_mp) == 0
        and hidden_in.shape[0] % (16 * lax.axis_size("dp")) == 0
    )
    chosen = fused if fits else shards
    return chosen(
        hidden_in, norm_gain, w_query, w_keyval, w_out, cache_slots, lengths, positions, slot_order
    )


def solution(mesh):
    placed = (
        P(None, "dp"),
        P("dp"),
        P("dp", "mp"),
        P("dp", "mp"),
        P("mp", "dp"),
        P(None, ("dp", "mp"), None, None, None, None),
        P(),
        P(),
        P(),
    )
    return jax.shard_map(
        dispatch, mesh=mesh, in_specs=placed, out_specs=P(None, "dp"), check_vma=False
    )
```

```python
import functools
import math

import jax
import jax.numpy as jnp
import numpy as np
from jax import lax
from jax.experimental import pallas as pl
from jax.experimental.pallas import tpu as pltpu
from jax.sharding import PartitionSpec as P

LAYERS = 2


norm_eps = 1e-05
rope_base = 500000.0


def rotate(values, at_positions):
    half_dim = values.shape[-1] // 2
    index_row = jnp.arange(half_dim, dtype=jnp.float32)
    frequency = jnp.exp(index_row * (-2.0 * math.log(rope_base) / values.shape[-1]))
    angles = at_positions.astype(jnp.float32)[:, None, None] * frequency
    cosines = jnp.cos(angles)
    sine_rows = jnp.sin(angles)
    first_half = values[..., :half_dim]
    second_half = values[..., half_dim:]
    return jnp.concatenate(
        [
            first_half * cosines - second_half * sine_rows,
            second_half * cosines + first_half * sine_rows,
        ],
        axis=-1,
    )


def attend(queries, fresh_keys, fresh_values, key_rows, values, slot_lengths):
    score_scale = 1.0 / math.sqrt(queries.shape[-1])
    scores = (
        jnp.einsum("rkgd,rktd->rkgt", queries, key_rows, preferred_element_type=jnp.float32)
        * score_scale
    )
    own_score = (
        jnp.einsum("rkgd,rkd->rkg", queries, fresh_keys, preferred_element_type=jnp.float32)
        * score_scale
    )
    positions_row = lax.broadcasted_iota(jnp.int32, (1, 1, 1, key_rows.shape[2]), 3)
    valid_keys = positions_row < slot_lengths[:, None, None, None]
    scores = jnp.where(valid_keys, scores, -jnp.inf)
    highest = jnp.maximum(jnp.max(scores, axis=-1), own_score)
    weights = jnp.exp(scores - highest[..., None])
    own_weight = jnp.exp(own_score - highest)
    denominator = jnp.sum(weights, axis=-1) + own_weight
    rounded = weights.astype(jnp.bfloat16)
    own_rounded = lax.optimization_barrier(own_weight.astype(jnp.bfloat16)).astype(jnp.float32)
    summed = jnp.einsum("rkgt,rktd->rkgd", rounded, values, preferred_element_type=jnp.float32)
    summed = summed + own_rounded[..., None] * fresh_values.astype(jnp.float32)[:, :, None, :]
    return (summed / denominator[..., None]).astype(jnp.bfloat16)


def shards(
    hidden_in, norm_gain, w_query, w_keyval, w_out, cache_slots, lengths, positions, slot_order
):
    total_rows = hidden_in.shape[0]
    data_count = lax.axis_size("dp")
    model_count = lax.axis_size("mp")
    owned_rows = cache_slots.shape[1]
    key_heads = cache_slots.shape[3]
    head_dim = cache_slots.shape[5]
    query_cols = w_query.shape[1]
    head_count = query_cols * model_count // head_dim
    group_size = head_count // key_heads
    model_width = hidden_in.shape[1] * data_count
    half_width = key_heads * head_dim
    inverse = (
        jnp.zeros((total_rows,), jnp.int32)
        .at[slot_order]
        .set(jnp.arange(total_rows, dtype=jnp.int32))
    )
    device_index = lax.axis_index("dp") * model_count + lax.axis_index("mp")
    slot_lengths = lax.dynamic_slice_in_dim(
        jnp.take(lengths, slot_order), device_index * owned_rows, owned_rows
    )
    slot_positions = lax.dynamic_slice_in_dim(
        jnp.take(positions, slot_order), device_index * owned_rows, owned_rows
    )
    gain_float = norm_gain.astype(jnp.float32)
    current = jnp.take(hidden_in, slot_order, axis=0)
    for layer_index in range(LAYERS):
        floats = current.astype(jnp.float32)
        squares = jnp.sum(floats * floats, axis=1)
        scaled = (floats * gain_float).astype(jnp.bfloat16)
        partial_value = jnp.concatenate(
            [
                jnp.dot(scaled, w_query, preferred_element_type=jnp.float32),
                jnp.dot(scaled, w_keyval, preferred_element_type=jnp.float32),
            ],
            axis=1,
        )
        summed = lax.psum_scatter(partial_value, "dp", scatter_dimension=0, tiled=True)
        square_sum = lax.psum_scatter(squares, "dp", scatter_dimension=0, tiled=True)
        inverse_rms = lax.rsqrt(square_sum / model_width + norm_eps)
        projected = summed * inverse_rms[:, None]
        arrived = lax.all_to_all(projected, "mp", split_axis=0, concat_axis=1, tiled=True)
        arrived = arrived.reshape(owned_rows, model_count, projected.shape[1])
        query_part = arrived[:, :, :query_cols].reshape(owned_rows, head_count, head_dim)
        keyval_part = arrived[:, :, query_cols:].reshape(owned_rows, 2 * half_width)
        queries = (
            rotate(query_part, slot_positions)
            .astype(jnp.bfloat16)
            .reshape(owned_rows, key_heads, group_size, head_dim)
        )
        fresh_keys = rotate(
            keyval_part[:, :half_width].reshape(owned_rows, key_heads, head_dim), slot_positions
        ).astype(jnp.bfloat16)
        fresh_values = (
            keyval_part[:, half_width:]
            .reshape(owned_rows, key_heads, head_dim)
            .astype(jnp.bfloat16)
        )
        layer_cache = cache_slots[layer_index]
        attended = attend(
            queries, fresh_keys, fresh_values, layer_cache[:, 0], layer_cache[:, 1], slot_lengths
        )
        attended = attended.reshape(owned_rows, head_count * head_dim)
        returned = lax.all_to_all(attended, "mp", split_axis=1, concat_axis=0, tiled=True)
        partial_out = jnp.dot(
            lax.all_gather(returned, "dp", axis=0, tiled=True),
            w_out,
            preferred_element_type=jnp.float32,
        )
        totals = lax.psum(partial_out, "mp")
        current = (floats + totals).astype(jnp.bfloat16)
    return jnp.take(current, inverse, axis=0)


LINK = jnp.bfloat16


def fused_kernel(
    sizes,
    slot_s,
    length_s,
    position_s,
    slot_row,
    frequency_ref,
    hidden_ref,
    gain_ref,
    wq_hbm,
    wkv_hbm,
    wo_hbm,
    cache_hbm,
    out_ref,
    wq,
    wkv,
    wo,
    cache,
    state,
    scaled,
    part_own,
    square_send,
    square_recv,
    part_send,
    part_recv,
    proj_send,
    proj_recv,
    query_buf,
    fresh_buf,
    att_buf,
    att_send,
    att_recv,
    att_rows,
    gathered,
    pair_send,
    pair_recv,
    out_all,
    load_sem,
    sq_ssem,
    sq_rsem,
    pa_ssem,
    pa_rsem,
    pr_ssem,
    pr_rsem,
    at_ssem,
    at_rsem,
    ga_ssem,
    ga_rsem,
    pq_ssem,
    pq_rsem,
    ou_ssem,
    ou_rsem,
    st_ssem,
    st_rsem,
):
    n_dp, n_mp, rows, width, query_cols, keyval_cols, owned, key_heads, head_dim = sizes
    band = rows // n_dp
    chunk = width // n_mp
    group = query_cols // head_dim
    block = keyval_cols
    blocks = (query_cols + keyval_cols) // block
    d = lax.axis_index("dp")
    m = lax.axis_index("mp")
    model_width = width * n_dp
    core = lax.rem(m, 2)
    chip = m // 2
    sibling = m + 1 - 2 * core
    n_chip = n_mp // 2
    half = n_mp // 2
    score_scale = 1.0 / math.sqrt(head_dim)

    loads = [
        pltpu.make_async_copy(wkv_hbm, wkv, load_sem.at[0]),
        pltpu.make_async_copy(wq_hbm, wq, load_sem.at[1]),
        pltpu.make_async_copy(cache_hbm.at[0], cache.at[0], load_sem.at[2]),
    ]
    for j in range(n_mp):
        loads.append(
            pltpu.make_async_copy(
                wo_hbm.at[:, pl.ds(j * chunk, chunk)], wo.at[j], load_sem.at[3 + j]
            )
        )
    for layer in range(1, LAYERS):
        loads.append(
            pltpu.make_async_copy(
                cache_hbm.at[layer], cache.at[layer], load_sem.at[2 + n_mp + layer]
            )
        )
    for one in loads:
        one.start()

    barrier = pltpu.get_barrier_semaphore()
    for k in range(1, n_dp):
        pl.semaphore_signal(
            barrier,
            inc=1,
            device_id={"dp": lax.rem(d + k, n_dp)},
            device_id_type=pl.DeviceIdType.MESH,
        )
    for k in range(1, n_mp):
        pl.semaphore_signal(
            barrier,
            inc=1,
            device_id={"mp": lax.rem(m + k, n_mp)},
            device_id_type=pl.DeviceIdType.MESH,
        )

    sublanes = lax.broadcasted_iota(jnp.int32, (rows, rows), 0)
    place = jnp.where(slot_row[...] == sublanes, 1.0, 0.0).astype(jnp.bfloat16)
    gains = gain_ref[...].astype(jnp.float32)
    for c in range(n_mp):
        state[0, c] = lax.dot_general(
            place,
            hidden_ref[:, c * chunk : (c + 1) * chunk],
            (((0,), (0,)), ((), ())),
            preferred_element_type=jnp.float32,
        ).astype(jnp.bfloat16)

    pl.semaphore_wait(barrier, n_dp - 1 + n_mp - 1)

    turns = []
    for r in range(owned):
        slot = slot_s[(d * n_mp + m) * owned + r]
        at = jnp.full((8, head_dim), position_s[slot], jnp.int32).astype(jnp.float32)
        angles = at * frequency_ref[...]
        lane = lax.broadcasted_iota(jnp.int32, (8, head_dim), 1)
        sines = jnp.sin(angles)
        turns.append(
            (jnp.cos(angles), jnp.where(lane < head_dim // 2, -sines, sines), length_s[slot])
        )

    sends = []

    def remote(src, dst, ssem, rsem, where):
        copy = pltpu.make_async_remote_copy(
            src_ref=src,
            dst_ref=dst,
            send_sem=ssem,
            recv_sem=rsem,
            device_id=where,
            device_id_type=pl.DeviceIdType.MESH,
        )
        copy.start()
        sends.append(copy)
        return copy

    arriving = []
    for layer in range(LAYERS):
        for copy in arriving:
            copy.wait_recv()
        squares = jnp.zeros((rows, 128), jnp.float32)
        for c in range(n_mp):
            floats = state[layer, c].astype(jnp.float32)
            for t in range(chunk // 128):
                piece = floats[:, t * 128 : (t + 1) * 128]
                at = c * (chunk // 128) + t
                scaled[:, at * 128 : (at + 1) * 128] = (piece * gains[at : at + 1]).astype(
                    jnp.bfloat16
                )
                squares = squares + piece * piece
        square_row = jnp.sum(squares, axis=1, keepdims=True)
        square_send[layer] = jnp.broadcast_to(square_row, (rows, 128)).reshape(n_dp, band, 128)
        square_copies = []
        for k in range(1, n_dp):
            to = lax.rem(d + k, n_dp)
            square_copies.append(
                remote(
                    square_send.at[layer, to],
                    square_recv.at[layer, k - 1],
                    sq_ssem.at[layer, k - 1],
                    sq_rsem.at[layer, k - 1],
                    {"dp": to},
                )
            )
        part_copies = []
        for b in range(blocks):
            if b == 0:
                if layer == 0:
                    loads[0].wait()
                weights = wkv[...]
            else:
                if layer == 0 and b == 1:
                    loads[1].wait()
                weights = wq[:, (b - 1) * block : b * block]
            product = jnp.dot(scaled[...], weights, preferred_element_type=jnp.float32)
            product = product.reshape(n_dp, band, block)
            part_own[b] = product
            part_send[layer, b] = product.astype(LINK)
            for k in range(1, n_dp):
                to = lax.rem(d + k, n_dp)
                part_copies.append(
                    remote(
                        part_send.at[layer, b, to],
                        part_recv.at[layer, b, k - 1],
                        pa_ssem.at[layer, b, k - 1],
                        pa_rsem.at[layer, b, k - 1],
                        {"dp": to},
                    )
                )
        for copy in square_copies:
            copy.wait_recv()
        square_sum = square_send[layer, d]
        for k in range(1, n_dp):
            square_sum = square_sum + square_recv[layer, k - 1]
        inverse_rms = lax.rsqrt(square_sum / model_width + norm_eps)[:, :1]
        for copy in part_copies:
            copy.wait_recv()
        for b in range(blocks):
            total = part_own[b, d]
            for k in range(1, n_dp):
                total = total + part_recv[layer, b, k - 1].astype(jnp.float32)
            total = total * inverse_rms
            start = query_cols if b == 0 else (b - 1) * block
            for j in range(n_mp):
                proj_send[layer, j, :, start : start + block] = total[
                    j * owned : (j + 1) * owned
                ]
        proj_copies = []
        for k in range(1, n_mp):
            to = lax.rem(m + k, n_mp)
            proj_copies.append(
                remote(
                    proj_send.at[layer, to],
                    proj_recv.at[layer, m],
                    pr_ssem.at[layer, k - 1],
                    pr_rsem.at[layer, k - 1],
                    {"mp": to},
                )
            )
        proj_recv[layer, m] = proj_send[layer, m]
        for copy in proj_copies:
            copy.wait_recv()

        if layer == 0:
            loads[2].wait()
        else:
            loads[2 + n_mp + layer].wait()
        for r in range(owned):
            cosines, sines, length = turns[r]

            def turned(x):
                return x * cosines + pltpu.roll(x, head_dim // 2, 1) * sines

            for g in range(group):
                query_buf[r, :, g, :] = turned(
                    proj_recv[layer, :, r, g * head_dim : (g + 1) * head_dim]
                )
            per = keyval_cols // head_dim
            key_sources = key_heads // per
            for t in range(per):
                start = query_cols + t * head_dim
                fresh = proj_recv[layer, :, r, start : start + head_dim]
                keys_fresh = turned(fresh)
                for source in range(n_mp):
                    kind = source // key_sources
                    head = (source % key_sources) * per + t
                    row = keys_fresh if kind == 0 else fresh
                    fresh_buf[r, kind, head : head + 1, :] = row[source : source + 1]
            queries = query_buf[r].astype(jnp.bfloat16)
            fresh_keys = fresh_buf[r, 0].astype(jnp.bfloat16).astype(jnp.float32)
            fresh_values = fresh_buf[r, 1].astype(jnp.bfloat16).astype(jnp.float32)
            key_rows = cache[layer, r, 0]
            value_rows = cache[layer, r, 1]
            scores = (
                lax.dot_general(
                    queries,
                    key_rows,
                    (((2,), (2,)), ((0,), (0,))),
                    preferred_element_type=jnp.float32,
                )
                * score_scale
            )
            own_score = (
                jnp.sum(
                    queries.astype(jnp.float32) * fresh_keys[:, None, :], axis=2, keepdims=True
                )
                * score_scale
            )
            at = lax.broadcasted_iota(jnp.int32, scores.shape, 2)
            scores = jnp.where(at < length, scores, -jnp.inf)
            highest = jnp.maximum(jnp.max(scores, axis=2, keepdims=True), own_score)
            weights = jnp.exp(scores - highest)
            own_weight = jnp.exp(own_score - highest)
            denominator = jnp.sum(weights, axis=2, keepdims=True) + own_weight
            summed = lax.dot_general(
                weights.astype(jnp.bfloat16),
                value_rows,
                (((2,), (1,)), ((0,), (0,))),
                preferred_element_type=jnp.float32,
            )
            own_rounded = own_weight.astype(jnp.bfloat16).astype(jnp.float32)
            summed = summed + own_rounded * fresh_values[:, None, :]
            att_buf[r] = summed / denominator
            for g in range(group):
                att_send[layer, :, r, g * head_dim : (g + 1) * head_dim] = att_buf[r, :, g, :]
        att_copies = []
        for k in range(1, n_mp):
            to = lax.rem(m + k, n_mp)
            att_copies.append(
                remote(
                    att_send.at[layer, to],
                    att_recv.at[layer, m],
                    at_ssem.at[layer, k - 1],
                    at_rsem.at[layer, k - 1],
                    {"mp": to},
                )
            )
        att_recv[layer, m] = att_send[layer, m]
        for copy in att_copies:
            copy.wait_recv()
        for j in range(n_mp):
            att_rows[j * owned : (j + 1) * owned, :] = att_recv[layer, j]
        gathered[layer, d] = att_rows[...].astype(jnp.bfloat16)
        gather_copies = []
        for k in range(1, n_dp):
            gather_copies.append(
                remote(
                    gathered.at[layer, d],
                    gathered.at[layer, d],
                    ga_ssem.at[layer, k - 1],
                    ga_rsem.at[layer, k - 1],
                    {"dp": lax.rem(d + k, n_dp)},
                )
            )
        for copy in gather_copies:
            copy.wait_recv()
        if layer == 0:
            for j in range(n_mp):
                loads[3 + j].wait()
        left = gathered[layer].reshape(rows, query_cols)
        pair_copies = []
        for q in range(half):
            pair_send[layer, q] = jnp.dot(
                left, wo[(1 - core) * half + q], preferred_element_type=jnp.float32
            )
            pair_copies.append(
                remote(
                    pair_send.at[layer, q],
                    pair_recv.at[layer, q],
                    pq_ssem.at[layer, q],
                    pq_rsem.at[layer, q],
                    {"mp": sibling},
                )
            )
        out_copies = []
        for q in range(half):
            product = jnp.dot(left, wo[core * half + q], preferred_element_type=jnp.float32)
            pair_copies[q].wait_recv()
            out_all[layer, chip, q] = (product + pair_recv[layer, q]).astype(LINK)
            for k in range(1, n_chip):
                out_copies.append(
                    remote(
                        out_all.at[layer, chip, q],
                        out_all.at[layer, chip, q],
                        ou_ssem.at[layer, q, k - 1],
                        ou_rsem.at[layer, q, k - 1],
                        {"mp": lax.rem(chip + k, n_chip) * 2 + core},
                    )
                )
        arriving = []
        for q in range(half):
            at = core * half + q
            total = state[layer, at].astype(jnp.float32)
            for k in range(1, n_chip):
                out_copies[q * (n_chip - 1) + k - 1].wait_recv()
            for c in range(n_chip):
                total = total + out_all[layer, c, q].astype(jnp.float32)
            state[layer + 1, at] = total.astype(jnp.bfloat16)
            arriving.append(
                remote(
                    state.at[layer + 1, at],
                    state.at[layer + 1, at],
                    st_ssem.at[layer, q],
                    st_rsem.at[layer, q],
                    {"mp": sibling},
                )
            )
    for copy in arriving:
        copy.wait_recv()
    for c in range(n_mp):
        out_ref[:, c * chunk : (c + 1) * chunk] = jnp.dot(
            place, state[LAYERS, c], preferred_element_type=jnp.float32
        ).astype(jnp.bfloat16)
    for copy in sends:
        copy.wait_send()


def fused(
    hidden_in, norm_gain, w_query, w_keyval, w_out, cache_slots, lengths, positions, slot_order
):
    n_dp = lax.axis_size("dp")
    n_mp = lax.axis_size("mp")
    rows, width = hidden_in.shape
    query_cols = w_query.shape[1]
    keyval_cols = w_keyval.shape[1]
    owned, key_heads, cache_rows, head_dim = (
        cache_slots.shape[1],
        cache_slots.shape[3],
        cache_slots.shape[4],
        cache_slots.shape[5],
    )
    group = query_cols // head_dim
    band = rows // n_dp
    chunk = width // n_mp
    blocks = (query_cols + keyval_cols) // keyval_cols
    index_row = np.arange(head_dim) % (head_dim // 2)
    frequency = np.exp(index_row * (-2.0 * math.log(rope_base) / head_dim))
    frequency = jnp.asarray(frequency[None].astype(np.float32))
    sizes = (n_dp, n_mp, rows, width, query_cols, keyval_cols, owned, key_heads, head_dim)
    vmem = pl.BlockSpec(memory_space=pltpu.VMEM)
    smem = pl.BlockSpec(memory_space=pltpu.SMEM)
    anywhere = pl.BlockSpec(memory_space=pl.ANY)
    f32, bf16 = jnp.float32, jnp.bfloat16
    dma = pltpu.SemaphoreType.DMA
    return pl.pallas_call(
        functools.partial(fused_kernel, sizes),
        out_shape=jax.ShapeDtypeStruct((rows, width), bf16),
        in_specs=[smem, smem, smem, vmem, vmem, vmem, vmem] + [anywhere] * 4,
        out_specs=vmem,
        scratch_shapes=[
            pltpu.VMEM(w_query.shape, bf16),
            pltpu.VMEM(w_keyval.shape, bf16),
            pltpu.VMEM((n_mp, query_cols, chunk), bf16),
            pltpu.VMEM(cache_slots.shape, bf16),
            pltpu.VMEM((LAYERS + 1, n_mp, rows, chunk), bf16),
            pltpu.VMEM((rows, width), bf16),
            pltpu.VMEM((blocks, n_dp, band, keyval_cols), f32),
            pltpu.VMEM((LAYERS, n_dp, band, 128), f32),
            pltpu.VMEM((LAYERS, n_dp - 1, band, 128), f32),
            pltpu.VMEM((LAYERS, blocks, n_dp, band, keyval_cols), LINK),
            pltpu.VMEM((LAYERS, blocks, n_dp - 1, band, keyval_cols), LINK),
            pltpu.VMEM((LAYERS, n_mp, owned, query_cols + keyval_cols), f32),
            pltpu.VMEM((LAYERS, n_mp, owned, query_cols + keyval_cols), f32),
            pltpu.VMEM((owned, n_mp, group, head_dim), f32),
            pltpu.VMEM((owned, 2, key_heads, head_dim), f32),
            pltpu.VMEM((owned, n_mp, group, head_dim), f32),
            pltpu.VMEM((LAYERS, n_mp, owned, query_cols), f32),
            pltpu.VMEM((LAYERS, n_mp, owned, query_cols), f32),
            pltpu.VMEM((band, query_cols), f32),
            pltpu.VMEM((LAYERS, n_dp, band, query_cols), bf16),
            pltpu.VMEM((LAYERS, n_mp // 2, rows, chunk), f32),
            pltpu.VMEM((LAYERS, n_mp // 2, rows, chunk), f32),
            pltpu.VMEM((LAYERS, n_mp // 2, n_mp // 2, rows, chunk), LINK),
            dma((2 + n_mp + LAYERS,)),
            dma((LAYERS, n_dp - 1)),
            dma((LAYERS, n_dp - 1)),
            dma((LAYERS, blocks, n_dp - 1)),
            dma((LAYERS, blocks, n_dp - 1)),
            dma((LAYERS, n_mp - 1)),
            dma((LAYERS, n_mp - 1)),
            dma((LAYERS, n_mp - 1)),
            dma((LAYERS, n_mp - 1)),
            dma((LAYERS, n_dp - 1)),
            dma((LAYERS, n_dp - 1)),
            dma((LAYERS, n_mp // 2)),
            dma((LAYERS, n_mp // 2)),
            dma((LAYERS, n_mp // 2, n_mp // 2 - 1)),
            dma((LAYERS, n_mp // 2, n_mp // 2 - 1)),
            dma((LAYERS, n_mp // 2)),
            dma((LAYERS, n_mp // 2)),
        ],
        compiler_params=pltpu.CompilerParams(
            collective_id=0, has_side_effects=True, vmem_limit_bytes=56 << 20
        ),
    )(
        slot_order,
        lengths,
        positions,
        slot_order.reshape(1, rows),
        frequency,
        hidden_in,
        norm_gain.reshape(width // 128, 128),
        w_query,
        w_keyval,
        w_out,
        cache_slots,
    )


def dispatch(
    hidden_in, norm_gain, w_query, w_keyval, w_out, cache_slots, lengths, positions, slot_order
):
    n_mp = lax.axis_size("mp")
    key_heads = cache_slots.shape[3]
    head_dim = cache_slots.shape[5]
    fits = (
        key_heads == n_mp
        and n_mp % 2 == 0
        and w_keyval.shape[1] % head_dim == 0
        and w_query.shape[1] % w_keyval.shape[1] == 0
        and hidden_in.shape[1] % (128 * n_mp) == 0
        and hidden_in.shape[0] % (16 * lax.axis_size("dp")) == 0
    )
    chosen = fused if fits else shards
    return chosen(
        hidden_in, norm_gain, w_query, w_keyval, w_out, cache_slots, lengths, positions, slot_order
    )


def solution(mesh):
    placed = (
        P(None, "dp"),
        P("dp"),
        P("dp", "mp"),
        P("dp", "mp"),
        P("mp", "dp"),
        P(None, ("dp", "mp"), None, None, None, None),
        P(),
        P(),
        P(),
    )
    return jax.shard_map(
        dispatch, mesh=mesh, in_specs=placed, out_specs=P(None, "dp"), check_vma=False
    )
```

```python
import functools
import math

import jax
import jax.numpy as jnp
import numpy as np
from jax import lax
from jax.experimental import pallas as pl
from jax.experimental.pallas import tpu as pltpu
from jax.sharding import PartitionSpec as P

LAYERS = 2


norm_eps = 1e-05
rope_base = 500000.0


def rotate(values, at_positions):
    half_dim = values.shape[-1] // 2
    index_row = jnp.arange(half_dim, dtype=jnp.float32)
    frequency = jnp.exp(index_row * (-2.0 * math.log(rope_base) / values.shape[-1]))
    angles = at_positions.astype(jnp.float32)[:, None, None] * frequency
    cosines = jnp.cos(angles)
    sine_rows = jnp.sin(angles)
    first_half = values[..., :half_dim]
    second_half = values[..., half_dim:]
    return jnp.concatenate(
        [
            first_half * cosines - second_half * sine_rows,
            second_half * cosines + first_half * sine_rows,
        ],
        axis=-1,
    )


def attend(queries, fresh_keys, fresh_values, key_rows, values, slot_lengths):
    score_scale = 1.0 / math.sqrt(queries.shape[-1])
    scores = (
        jnp.einsum("rkgd,rktd->rkgt", queries, key_rows, preferred_element_type=jnp.float32)
        * score_scale
    )
    own_score = (
        jnp.einsum("rkgd,rkd->rkg", queries, fresh_keys, preferred_element_type=jnp.float32)
        * score_scale
    )
    positions_row = lax.broadcasted_iota(jnp.int32, (1, 1, 1, key_rows.shape[2]), 3)
    valid_keys = positions_row < slot_lengths[:, None, None, None]
    scores = jnp.where(valid_keys, scores, -jnp.inf)
    highest = jnp.maximum(jnp.max(scores, axis=-1), own_score)
    weights = jnp.exp(scores - highest[..., None])
    own_weight = jnp.exp(own_score - highest)
    denominator = jnp.sum(weights, axis=-1) + own_weight
    rounded = weights.astype(jnp.bfloat16)
    own_rounded = lax.optimization_barrier(own_weight.astype(jnp.bfloat16)).astype(jnp.float32)
    summed = jnp.einsum("rkgt,rktd->rkgd", rounded, values, preferred_element_type=jnp.float32)
    summed = summed + own_rounded[..., None] * fresh_values.astype(jnp.float32)[:, :, None, :]
    return (summed / denominator[..., None]).astype(jnp.bfloat16)


def shards(
    hidden_in, norm_gain, w_query, w_keyval, w_out, cache_slots, lengths, positions, slot_order
):
    total_rows = hidden_in.shape[0]
    data_count = lax.axis_size("dp")
    model_count = lax.axis_size("mp")
    owned_rows = cache_slots.shape[1]
    key_heads = cache_slots.shape[3]
    head_dim = cache_slots.shape[5]
    query_cols = w_query.shape[1]
    head_count = query_cols * model_count // head_dim
    group_size = head_count // key_heads
    model_width = hidden_in.shape[1] * data_count
    half_width = key_heads * head_dim
    inverse = (
        jnp.zeros((total_rows,), jnp.int32)
        .at[slot_order]
        .set(jnp.arange(total_rows, dtype=jnp.int32))
    )
    device_index = lax.axis_index("dp") * model_count + lax.axis_index("mp")
    slot_lengths = lax.dynamic_slice_in_dim(
        jnp.take(lengths, slot_order), device_index * owned_rows, owned_rows
    )
    slot_positions = lax.dynamic_slice_in_dim(
        jnp.take(positions, slot_order), device_index * owned_rows, owned_rows
    )
    gain_float = norm_gain.astype(jnp.float32)
    current = jnp.take(hidden_in, slot_order, axis=0)
    for layer_index in range(LAYERS):
        floats = current.astype(jnp.float32)
        squares = jnp.sum(floats * floats, axis=1)
        scaled = (floats * gain_float).astype(jnp.bfloat16)
        partial_value = jnp.concatenate(
            [
                jnp.dot(scaled, w_query, preferred_element_type=jnp.float32),
                jnp.dot(scaled, w_keyval, preferred_element_type=jnp.float32),
            ],
            axis=1,
        )
        summed = lax.psum_scatter(partial_value, "dp", scatter_dimension=0, tiled=True)
        square_sum = lax.psum_scatter(squares, "dp", scatter_dimension=0, tiled=True)
        inverse_rms = lax.rsqrt(square_sum / model_width + norm_eps)
        projected = summed * inverse_rms[:, None]
        arrived = lax.all_to_all(projected, "mp", split_axis=0, concat_axis=1, tiled=True)
        arrived = arrived.reshape(owned_rows, model_count, projected.shape[1])
        query_part = arrived[:, :, :query_cols].reshape(owned_rows, head_count, head_dim)
        keyval_part = arrived[:, :, query_cols:].reshape(owned_rows, 2 * half_width)
        queries = (
            rotate(query_part, slot_positions)
            .astype(jnp.bfloat16)
            .reshape(owned_rows, key_heads, group_size, head_dim)
        )
        fresh_keys = rotate(
            keyval_part[:, :half_width].reshape(owned_rows, key_heads, head_dim), slot_positions
        ).astype(jnp.bfloat16)
        fresh_values = (
            keyval_part[:, half_width:]
            .reshape(owned_rows, key_heads, head_dim)
            .astype(jnp.bfloat16)
        )
        layer_cache = cache_slots[layer_index]
        attended = attend(
            queries, fresh_keys, fresh_values, layer_cache[:, 0], layer_cache[:, 1], slot_lengths
        )
        attended = attended.reshape(owned_rows, head_count * head_dim)
        returned = lax.all_to_all(attended, "mp", split_axis=1, concat_axis=0, tiled=True)
        partial_out = jnp.dot(
            lax.all_gather(returned, "dp", axis=0, tiled=True),
            w_out,
            preferred_element_type=jnp.float32,
        )
        totals = lax.psum(partial_out, "mp")
        current = (floats + totals).astype(jnp.bfloat16)
    return jnp.take(current, inverse, axis=0)


LINK = jnp.bfloat16


def fused_kernel(
    sizes,
    slot_s,
    length_s,
    position_s,
    slot_row,
    frequency_ref,
    hidden_ref,
    gain_ref,
    wq_hbm,
    wkv_hbm,
    wo_hbm,
    cache_hbm,
    out_ref,
    wq,
    wkv,
    wo,
    cache,
    state,
    scaled,
    part_own,
    square_send,
    square_recv,
    part_send,
    part_recv,
    proj_send,
    proj_recv,
    query_buf,
    fresh_buf,
    att_buf,
    att_send,
    att_pair,
    att_quad,
    att_rows,
    gathered,
    pair_send,
    pair_recv,
    out_all,
    load_sem,
    sq_ssem,
    sq_rsem,
    pa_ssem,
    pa_rsem,
    pr_ssem,
    pr_rsem,
    as_ssem,
    as_rsem,
    ga_ssem,
    ga_rsem,
    pq_ssem,
    pq_rsem,
    ou_ssem,
    ou_rsem,
    st_ssem,
    st_rsem,
):
    n_dp, n_mp, rows, width, query_cols, keyval_cols, owned, key_heads, head_dim = sizes
    band = rows // n_dp
    chunk = width // n_mp
    group = query_cols // head_dim
    block = keyval_cols
    blocks = (query_cols + keyval_cols) // block
    d = lax.axis_index("dp")
    m = lax.axis_index("mp")
    model_width = width * n_dp
    core = lax.rem(m, 2)
    chip = m // 2
    sibling = m + 1 - 2 * core
    n_chip = n_mp // 2
    half = n_mp // 2
    score_scale = 1.0 / math.sqrt(head_dim)

    loads = [
        pltpu.make_async_copy(wkv_hbm, wkv, load_sem.at[0]),
        pltpu.make_async_copy(wq_hbm, wq, load_sem.at[1]),
        pltpu.make_async_copy(cache_hbm.at[0], cache.at[0], load_sem.at[2]),
    ]
    for j in range(n_mp):
        loads.append(
            pltpu.make_async_copy(
                wo_hbm.at[:, pl.ds(j * chunk, chunk)], wo.at[j], load_sem.at[3 + j]
            )
        )
    for layer in range(1, LAYERS):
        loads.append(
            pltpu.make_async_copy(
                cache_hbm.at[layer], cache.at[layer], load_sem.at[2 + n_mp + layer]
            )
        )
    for one in loads:
        one.start()

    barrier = pltpu.get_barrier_semaphore()
    peers = [
        {"dp": lax.rem(d + kd, n_dp), "mp": lax.rem(chip + kc, n_chip) * 2 + core}
        for kd in range(n_dp)
        for kc in range(n_chip)
        if kd or kc
    ]
    peers += [{"mp": lax.rem(chip + kc, n_chip) * 2 + 1 - core} for kc in range(n_chip)]
    for peer in peers:
        pl.semaphore_signal(
            barrier, inc=1, device_id=peer, device_id_type=pl.DeviceIdType.MESH
        )

    sublanes = lax.broadcasted_iota(jnp.int32, (rows, rows), 0)
    place = jnp.where(slot_row[...] == sublanes, 1.0, 0.0).astype(jnp.bfloat16)
    gains = gain_ref[...].astype(jnp.float32)
    for c in range(n_mp):
        state[0, c] = lax.dot_general(
            place,
            hidden_ref[:, c * chunk : (c + 1) * chunk],
            (((0,), (0,)), ((), ())),
            preferred_element_type=jnp.float32,
        ).astype(jnp.bfloat16)

    turns = []
    for r in range(owned):
        slot = slot_s[(d * n_mp + m) * owned + r]
        at = jnp.full((8, head_dim), position_s[slot], jnp.int32).astype(jnp.float32)
        angles = at * frequency_ref[...]
        lane = lax.broadcasted_iota(jnp.int32, (8, head_dim), 1)
        sines = jnp.sin(angles)
        turns.append(
            (jnp.cos(angles), jnp.where(lane < head_dim // 2, -sines, sines), length_s[slot])
        )

    pl.semaphore_wait(barrier, n_chip + n_dp * n_chip - 1)

    sends = []

    def remote(src, dst, ssem, rsem, where):
        copy = pltpu.make_async_remote_copy(
            src_ref=src,
            dst_ref=dst,
            send_sem=ssem,
            recv_sem=rsem,
            device_id=where,
            device_id_type=pl.DeviceIdType.MESH,
        )
        copy.start()
        sends.append(copy)
        return copy

    arriving = []
    for layer in range(LAYERS):
        for copy in arriving:
            copy.wait_recv()
        squares = jnp.zeros((rows, 128), jnp.float32)
        for c in range(n_mp):
            floats = state[layer, c].astype(jnp.float32)
            for t in range(chunk // 128):
                piece = floats[:, t * 128 : (t + 1) * 128]
                at = c * (chunk // 128) + t
                scaled[:, at * 128 : (at + 1) * 128] = (piece * gains[at : at + 1]).astype(
                    jnp.bfloat16
                )
                squares = squares + piece * piece
        square_row = jnp.sum(squares, axis=1, keepdims=True)
        square_send[layer] = jnp.broadcast_to(square_row, (rows, 128)).reshape(n_dp, band, 128)
        square_copies = []
        for k in range(1, n_dp):
            to = lax.rem(d + k, n_dp)
            square_copies.append(
                remote(
                    square_send.at[layer, to],
                    square_recv.at[layer, k - 1],
                    sq_ssem.at[layer, k - 1],
                    sq_rsem.at[layer, k - 1],
                    {"dp": to},
                )
            )
        part_copies = []
        for b in range(blocks):
            if b == 0:
                if layer == 0:
                    loads[0].wait()
                weights = wkv[...]
            else:
                if layer == 0 and b == 1:
                    loads[1].wait()
                weights = wq[:, (b - 1) * block : b * block]
            product = jnp.dot(scaled[...], weights, preferred_element_type=jnp.float32)
            product = product.reshape(n_dp, band, block)
            part_own[b] = product
            part_send[layer, b] = product.astype(LINK)
            for k in range(1, n_dp):
                to = lax.rem(d + k, n_dp)
                part_copies.append(
                    remote(
                        part_send.at[layer, b, to],
                        part_recv.at[layer, b, k - 1],
                        pa_ssem.at[layer, b, k - 1],
                        pa_rsem.at[layer, b, k - 1],
                        {"dp": to},
                    )
                )
        for copy in square_copies:
            copy.wait_recv()
        square_sum = square_send[layer, d]
        for k in range(1, n_dp):
            square_sum = square_sum + square_recv[layer, k - 1]
        inverse_rms = lax.rsqrt(square_sum / model_width + norm_eps)[:, :1]
        for copy in part_copies:
            copy.wait_recv()
        for b in range(blocks):
            total = part_own[b, d]
            for k in range(1, n_dp):
                total = total + part_recv[layer, b, k - 1].astype(jnp.float32)
            total = total * inverse_rms
            start = query_cols if b == 0 else (b - 1) * block
            for j in range(n_mp):
                proj_send[layer, j, :, start : start + block] = total[
                    j * owned : (j + 1) * owned
                ]
        proj_copies = []
        for k in range(1, n_mp):
            to = lax.rem(m + k, n_mp)
            proj_copies.append(
                remote(
                    proj_send.at[layer, to],
                    proj_recv.at[layer, m],
                    pr_ssem.at[layer, k - 1],
                    pr_rsem.at[layer, k - 1],
                    {"mp": to},
                )
            )
        proj_recv[layer, m] = proj_send[layer, m]
        for copy in proj_copies:
            copy.wait_recv()

        if layer == 0:
            loads[2].wait()
        else:
            loads[2 + n_mp + layer].wait()
        for r in range(owned):
            cosines, sines, length = turns[r]

            def turned(x):
                return x * cosines + pltpu.roll(x, head_dim // 2, 1) * sines

            for g in range(group):
                query_buf[r, :, g, :] = turned(
                    proj_recv[layer, :, r, g * head_dim : (g + 1) * head_dim]
                )
            per = keyval_cols // head_dim
            key_sources = key_heads // per
            for t in range(per):
                start = query_cols + t * head_dim
                fresh = proj_recv[layer, :, r, start : start + head_dim]
                keys_fresh = turned(fresh)
                for source in range(n_mp):
                    kind = source // key_sources
                    head = (source % key_sources) * per + t
                    row = keys_fresh if kind == 0 else fresh
                    fresh_buf[r, kind, head : head + 1, :] = row[source : source + 1]
            queries = query_buf[r].astype(jnp.bfloat16)
            fresh_keys = fresh_buf[r, 0].astype(jnp.bfloat16).astype(jnp.float32)
            fresh_values = fresh_buf[r, 1].astype(jnp.bfloat16).astype(jnp.float32)
            key_rows = cache[layer, r, 0]
            value_rows = cache[layer, r, 1]
            scores = (
                lax.dot_general(
                    queries,
                    key_rows,
                    (((2,), (2,)), ((0,), (0,))),
                    preferred_element_type=jnp.float32,
                )
                * score_scale
            )
            own_score = (
                jnp.sum(
                    queries.astype(jnp.float32) * fresh_keys[:, None, :], axis=2, keepdims=True
                )
                * score_scale
            )
            at = lax.broadcasted_iota(jnp.int32, scores.shape, 2)
            scores = jnp.where(at < length, scores, -jnp.inf)
            highest = jnp.maximum(jnp.max(scores, axis=2, keepdims=True), own_score)
            weights = jnp.exp(scores - highest)
            own_weight = jnp.exp(own_score - highest)
            denominator = jnp.sum(weights, axis=2, keepdims=True) + own_weight
            summed = lax.dot_general(
                weights.astype(jnp.bfloat16),
                value_rows,
                (((2,), (1,)), ((0,), (0,))),
                preferred_element_type=jnp.float32,
            )
            own_rounded = own_weight.astype(jnp.bfloat16).astype(jnp.float32)
            summed = summed + own_rounded * fresh_values[:, None, :]
            att_buf[r] = (summed / denominator).reshape(n_chip, 2, group, head_dim)
            for g in range(group):
                for e in range(2):
                    att_send[layer, e, :, r, g * head_dim : (g + 1) * head_dim] = att_buf[
                        r, :, e, g, :
                    ]
        pair = remote(
            att_send.at[layer, 1 - core],
            att_pair.at[layer],
            as_ssem.at[layer],
            as_rsem.at[layer],
            {"mp": sibling},
        )
        pair.wait_recv()
        gather_copies = []
        for kc in list(range(1, n_chip)) + [0]:
            to_chip = lax.rem(chip + kc, n_chip)
            mine = att_send[layer, core, to_chip]
            other = att_pair[layer, to_chip]
            att_quad[layer, kc, 0] = jnp.where(core == 0, mine, other).astype(jnp.bfloat16)
            att_quad[layer, kc, 1] = jnp.where(core == 0, other, mine).astype(jnp.bfloat16)
            for kd in range(n_dp):
                if kc or kd:
                    gather_copies.append(
                        remote(
                            att_quad.at[layer, kc],
                            gathered.at[layer, d, chip],
                            ga_ssem.at[layer, kc, kd],
                            ga_rsem.at[layer, kc, kd],
                            {"dp": lax.rem(d + kd, n_dp), "mp": to_chip * 2 + core},
                        )
                    )
        gathered[layer, d, chip] = att_quad[layer, 0]
        for copy in gather_copies:
            copy.wait_recv()
        for i in range(n_dp):
            for c in range(n_chip):
                for e in range(2):
                    at = ((i * n_chip + c) * 2 + e) * owned
                    att_rows[at : at + owned, :] = gathered[layer, i, c, e].astype(jnp.float32)
        if layer == 0:
            for j in range(n_mp):
                loads[3 + j].wait()
        left = att_rows[...].astype(jnp.bfloat16)
        pair_copies = []
        for q in range(half):
            pair_send[layer, q] = jnp.dot(
                left, wo[(1 - core) * half + q], preferred_element_type=jnp.float32
            )
            pair_copies.append(
                remote(
                    pair_send.at[layer, q],
                    pair_recv.at[layer, q],
                    pq_ssem.at[layer, q],
                    pq_rsem.at[layer, q],
                    {"mp": sibling},
                )
            )
        out_copies = []
        for q in range(half):
            product = jnp.dot(left, wo[core * half + q], preferred_element_type=jnp.float32)
            pair_copies[q].wait_recv()
            out_all[layer, chip, q] = (product + pair_recv[layer, q]).astype(LINK)
            for k in range(1, n_chip):
                out_copies.append(
                    remote(
                        out_all.at[layer, chip, q],
                        out_all.at[layer, chip, q],
                        ou_ssem.at[layer, q, k - 1],
                        ou_rsem.at[layer, q, k - 1],
                        {"mp": lax.rem(chip + k, n_chip) * 2 + core},
                    )
                )
        arriving = []
        for q in range(half):
            at = core * half + q
            total = state[layer, at].astype(jnp.float32)
            for k in range(1, n_chip):
                out_copies[q * (n_chip - 1) + k - 1].wait_recv()
            for c in range(n_chip):
                total = total + out_all[layer, c, q].astype(jnp.float32)
            state[layer + 1, at] = total.astype(jnp.bfloat16)
            arriving.append(
                remote(
                    state.at[layer + 1, at],
                    state.at[layer + 1, at],
                    st_ssem.at[layer, q],
                    st_rsem.at[layer, q],
                    {"mp": sibling},
                )
            )
    for copy in arriving:
        copy.wait_recv()
    for c in range(n_mp):
        out_ref[:, c * chunk : (c + 1) * chunk] = jnp.dot(
            place, state[LAYERS, c], preferred_element_type=jnp.float32
        ).astype(jnp.bfloat16)
    for copy in sends:
        copy.wait_send()


def fused(
    hidden_in, norm_gain, w_query, w_keyval, w_out, cache_slots, lengths, positions, slot_order
):
    n_dp = lax.axis_size("dp")
    n_mp = lax.axis_size("mp")
    rows, width = hidden_in.shape
    query_cols = w_query.shape[1]
    keyval_cols = w_keyval.shape[1]
    owned, key_heads, cache_rows, head_dim = (
        cache_slots.shape[1],
        cache_slots.shape[3],
        cache_slots.shape[4],
        cache_slots.shape[5],
    )
    group = query_cols // head_dim
    band = rows // n_dp
    chunk = width // n_mp
    blocks = (query_cols + keyval_cols) // keyval_cols
    index_row = np.arange(head_dim) % (head_dim // 2)
    frequency = np.exp(index_row * (-2.0 * math.log(rope_base) / head_dim))
    frequency = jnp.asarray(frequency[None].astype(np.float32))
    sizes = (n_dp, n_mp, rows, width, query_cols, keyval_cols, owned, key_heads, head_dim)
    vmem = pl.BlockSpec(memory_space=pltpu.VMEM)
    smem = pl.BlockSpec(memory_space=pltpu.SMEM)
    anywhere = pl.BlockSpec(memory_space=pl.ANY)
    f32, bf16 = jnp.float32, jnp.bfloat16
    dma = pltpu.SemaphoreType.DMA
    return pl.pallas_call(
        functools.partial(fused_kernel, sizes),
        out_shape=jax.ShapeDtypeStruct((rows, width), bf16),
        in_specs=[smem, smem, smem, vmem, vmem, vmem, vmem] + [anywhere] * 4,
        out_specs=vmem,
        scratch_shapes=[
            pltpu.VMEM(w_query.shape, bf16),
            pltpu.VMEM(w_keyval.shape, bf16),
            pltpu.VMEM((n_mp, query_cols, chunk), bf16),
            pltpu.VMEM(cache_slots.shape, bf16),
            pltpu.VMEM((LAYERS + 1, n_mp, rows, chunk), bf16),
            pltpu.VMEM((rows, width), bf16),
            pltpu.VMEM((blocks, n_dp, band, keyval_cols), f32),
            pltpu.VMEM((LAYERS, n_dp, band, 128), f32),
            pltpu.VMEM((LAYERS, n_dp - 1, band, 128), f32),
            pltpu.VMEM((LAYERS, blocks, n_dp, band, keyval_cols), LINK),
            pltpu.VMEM((LAYERS, blocks, n_dp - 1, band, keyval_cols), LINK),
            pltpu.VMEM((LAYERS, n_mp, owned, query_cols + keyval_cols), f32),
            pltpu.VMEM((LAYERS, n_mp, owned, query_cols + keyval_cols), f32),
            pltpu.VMEM((owned, n_mp, group, head_dim), f32),
            pltpu.VMEM((owned, 2, key_heads, head_dim), f32),
            pltpu.VMEM((owned, n_mp // 2, 2, group, head_dim), f32),
            pltpu.VMEM((LAYERS, 2, n_mp // 2, owned, query_cols), f32),
            pltpu.VMEM((LAYERS, n_mp // 2, owned, query_cols), f32),
            pltpu.VMEM((LAYERS, n_mp // 2, 2, owned, query_cols), bf16),
            pltpu.VMEM((rows, query_cols), f32),
            pltpu.VMEM((LAYERS, n_dp, n_mp // 2, 2, owned, query_cols), bf16),
            pltpu.VMEM((LAYERS, n_mp // 2, rows, chunk), f32),
            pltpu.VMEM((LAYERS, n_mp // 2, rows, chunk), f32),
            pltpu.VMEM((LAYERS, n_mp // 2, n_mp // 2, rows, chunk), LINK),
            dma((2 + n_mp + LAYERS,)),
            dma((LAYERS, n_dp - 1)),
            dma((LAYERS, n_dp - 1)),
            dma((LAYERS, blocks, n_dp - 1)),
            dma((LAYERS, blocks, n_dp - 1)),
            dma((LAYERS, n_mp - 1)),
            dma((LAYERS, n_mp - 1)),
            dma((LAYERS,)),
            dma((LAYERS,)),
            dma((LAYERS, n_mp // 2, n_dp)),
            dma((LAYERS, n_mp // 2, n_dp)),
            dma((LAYERS, n_mp // 2)),
            dma((LAYERS, n_mp // 2)),
            dma((LAYERS, n_mp // 2, n_mp // 2 - 1)),
            dma((LAYERS, n_mp // 2, n_mp // 2 - 1)),
            dma((LAYERS, n_mp // 2)),
            dma((LAYERS, n_mp // 2)),
        ],
        compiler_params=pltpu.CompilerParams(
            collective_id=0, has_side_effects=True, vmem_limit_bytes=56 << 20
        ),
    )(
        slot_order,
        lengths,
        positions,
        slot_order.reshape(1, rows),
        frequency,
        hidden_in,
        norm_gain.reshape(width // 128, 128),
        w_query,
        w_keyval,
        w_out,
        cache_slots,
    )


def dispatch(
    hidden_in, norm_gain, w_query, w_keyval, w_out, cache_slots, lengths, positions, slot_order
):
    n_mp = lax.axis_size("mp")
    key_heads = cache_slots.shape[3]
    head_dim = cache_slots.shape[5]
    fits = (
        key_heads == n_mp
        and n_mp % 2 == 0
        and w_keyval.shape[1] % head_dim == 0
        and w_query.shape[1] % w_keyval.shape[1] == 0
        and hidden_in.shape[1] % (128 * n_mp) == 0
        and hidden_in.shape[0] % (16 * lax.axis_size("dp")) == 0
    )
    chosen = fused if fits else shards
    return chosen(
        hidden_in, norm_gain, w_query, w_keyval, w_out, cache_slots, lengths, positions, slot_order
    )


def solution(mesh):
    placed = (
        P(None, "dp"),
        P("dp"),
        P("dp", "mp"),
        P("dp", "mp"),
        P("mp", "dp"),
        P(None, ("dp", "mp"), None, None, None, None),
        P(),
        P(),
        P(),
    )
    return jax.shard_map(
        dispatch, mesh=mesh, in_specs=placed, out_specs=P(None, "dp"), check_vma=False
    )
```
